32 devices in a mesh: groups: 2 (over y), row: 4 (over z), col: 4 (over x, core).
Axes of the slice: x: 2, y: 2, z: 4, core: 2. Of those that a mesh axis runs over, the one named last changes fastest.
Arguments:
- green_starting_blocks: float32 [4, 128, 2048], P('groups', None, ('row', 'col')), parts along dimension 0, may hold values from -3 to 3
- fit_vectors: bfloat16 [256, 4096], P('groups'), parts along dimension 0, may hold values from -0.75 to 0.75
- history: bfloat16 [4, 2048, 2048], P('groups', 'row', 'col'), parts along dimension 0, may hold values from -0.125 to 0.125
Outputs:
- green_final: float32 [4, 128, 2048], P('groups', None, ('row', 'col')), parts along dimension 0
The draws below stay inside these ranges and needn't reach their ends.
There are 2 independent parts, one for each index of `groups`. The reference program is written for one: setup_inputs(seed, part) draws one part's arguments, and reference() takes and returns one part's arrays. A program takes and returns all parts, laid end to end along the dimension named above; each array names one. Nothing has to cross between parts.
All inputs are finite; a program needn't handle non-finite values.
Results may differ from the reference program's by a relative error of at most 0.03.
Values may be sent and summed in bfloat16 or wider, within the bound.
A program may use at most 128 MiB of HBM per device.

```python
import jax
import jax.numpy as jnp
from jax import lax

NO = 64
NAUX = 128
NEW = 2
ITERS = 2
PAST = 32
SLICE_ROWS = 128
ORDER = 2048


def strengthened(array, own_key, source, target, blocks, factor):
    owner, partner = [(jnp.arange(array.shape[axis_at]) // (array.shape[axis_at] // blocks)).reshape([-1 if axis == axis_at else 1 for axis in range(array.ndim)]) for axis_at in (source, target)]
    chosen = jax.random.permutation(own_key, blocks)[partner]
    strong = (owner == chosen) | (owner == (partner + blocks // 2) % blocks)
    return jnp.where(strong, factor * array, array)


def steps_of(key, shape, pieces, smallest, high):
    gain = 1.0
    for dim, blocks in pieces:
        steps = jax.random.uniform(jax.random.fold_in(jax.random.fold_in(key, 6), dim), (blocks,), jnp.float32, smallest / len(pieces), high / len(pieces))
        gain = gain * jnp.repeat(jnp.exp(steps), shape[dim] // blocks).reshape((-1,) + (1,) * (len(shape) - 1 - dim))
    return gain


def gaussian(rng, extent, spread, limit, split=(), kind=jnp.bfloat16):
    entries = spread * jax.random.normal(rng, extent, jnp.float32)
    if split:
        entries = entries * steps_of(rng, extent, split, -0.22, 0.18)
    return jnp.clip(entries, -limit, limit).astype(kind)


def bell_draw_with(own_key, extent, deviation, bound, split, heavy, kind=jnp.bfloat16):
    array = deviation * jax.random.normal(own_key, extent, jnp.float32)
    if split:
        array = array * steps_of(own_key, extent, split, -0.22, 0.18)
    return jnp.clip(strengthened(array, jax.random.fold_in(own_key, 3), *heavy), -bound, bound).astype(kind)


def setup_inputs(seed: int = 0, part: int = 0) -> dict:
    seeds = jax.random.split(jax.random.key(seed), 4)
    part_splits = jax.random.split(jax.random.fold_in(seeds[3], part), 4)
    return {
        "green_starting_blocks": gaussian(part_splits[0], (2, SLICE_ROWS, ORDER), 0.5, 3.0, ((2, 16),), jnp.float32),
        "fit_vectors": gaussian(part_splits[1], (NAUX, NO * NO), NO ** -0.5, 0.75),
        "history": bell_draw_with(part_splits[2], (2, ORDER, ORDER), (2 * ORDER) ** -0.5, 0.125, ((1, 4), (2, 4)), (1, 2, 4, 2.0)),
    }


def pair_self_energy(pair_blocks, fit_vectors):
    pair_count = pair_blocks.shape[1]
    orbitals = pair_blocks.shape[2]
    aux_count = fit_vectors.shape[0]
    lowered = pair_blocks.astype(jnp.bfloat16)
    fit_basis = fit_vectors.reshape(aux_count * orbitals, orbitals)
    inner_side = jnp.transpose(lowered, (2, 0, 1, 3)).reshape(orbitals, 2 * pair_count * orbitals)
    left_prod = jnp.dot(fit_basis, inner_side, preferred_element_type=jnp.float32).astype(jnp.bfloat16)
    left_prod = left_prod.reshape(aux_count, orbitals, 2, pair_count, orbitals)
    fit_turned = jnp.transpose(fit_vectors.reshape(aux_count, orbitals, orbitals), (1, 0, 2)).reshape(orbitals, aux_count * orbitals)
    right_prod = jnp.dot(lowered.reshape(2 * pair_count * orbitals, orbitals), fit_turned, preferred_element_type=jnp.float32).astype(jnp.bfloat16)
    right_prod = right_prod.reshape(2, pair_count, orbitals, aux_count, orbitals)
    bubble = jnp.einsum("picnk,cniqk->npq", left_prod.astype(jnp.float32), right_prod.astype(jnp.float32)) / orbitals
    bubble = bubble.astype(jnp.bfloat16)
    screened = jnp.einsum("npq,qm->npm", bubble.astype(jnp.float32), fit_vectors.astype(jnp.float32)).astype(jnp.bfloat16)
    screened = screened.reshape(pair_count, aux_count, orbitals, orbitals)
    scale_factor = (aux_count * orbitals) ** -0.5
    energy = jnp.einsum("picnl,nplj->cnij", left_prod.astype(jnp.float32), screened.astype(jnp.float32)) * scale_factor
    return energy.astype(jnp.bfloat16)


def reference(green_starting_blocks, fit_vectors, history):
    green_current = green_starting_blocks

    def per_time(time_block):
        return pair_self_energy(time_block, fit_vectors)

    for iteration in range(ITERS):
        time_blocks = green_current.reshape(2, NEW, NO, PAST, NO).transpose(3, 0, 1, 2, 4)
        energies = lax.map(per_time, time_blocks)
        self_energy = energies.transpose(1, 2, 3, 0, 4).reshape(2, SLICE_ROWS, ORDER)
        stacked = self_energy.reshape(2 * SLICE_ROWS, ORDER)
        real_half = jnp.dot(stacked, history[0], preferred_element_type=jnp.float32)
        imaginary_half = jnp.dot(stacked, history[1], preferred_element_type=jnp.float32)
        collision_real = real_half[:SLICE_ROWS] - imaginary_half[SLICE_ROWS:]
        collision_imaginary = imaginary_half[:SLICE_ROWS] + real_half[SLICE_ROWS:]
        green_current = green_starting_blocks + jnp.stack([collision_real, collision_imaginary])
    return green_current
```

```python
import functools

import jax
import jax.numpy as jnp
from jax import lax
from jax.experimental import pallas as pl
from jax.experimental.pallas import tpu as pltpu
from jax.sharding import PartitionSpec as P

NO = 64
NEW = 2
ITERS = 2
PITCH = NO + 8
F32 = jnp.float32
BF16 = jnp.bfloat16
MESH = pl.DeviceIdType.MESH
VMEM = pl.BlockSpec(memory_space=pltpu.VMEM)


def mm(a, b):
    return jnp.dot(a, b, preferred_element_type=F32)


def mm_nt(a, b):
    return lax.dot_general(a, b, (((1,), (1,)), ((), ())), preferred_element_type=F32)


def prep_kernel(fit_ref, inner_ref, outer_ref, turned):
    aux = fit_ref.shape[0]
    for pair in range(NO // 2):
        block = fit_ref[:, pair * 2 * NO : (pair + 1) * 2 * NO].astype(F32).T
        for half in range(2):
            i = 2 * pair + half
            piece = block[half * NO : (half + 1) * NO]
            inner_ref[:, i * aux : (i + 1) * aux] = piece.astype(BF16)
            turned[i * PITCH : i * PITCH + NO, :] = piece
    for j in range(NO):
        piece = turned[pl.ds(j, NO, stride=PITCH), :]
        outer_ref[j * aux : (j + 1) * aux, :] = piece.T.astype(BF16)


def energy_kernel(green_ref, fit_ref, inner_ref, outer_ref, energy_ref, g_in, g_out, spread, m_ref, k_ref, pi_ref, w_ref):
    aux = fit_ref.shape[0]
    times = green_ref.shape[2] // NO
    pairs = NEW * times
    width = 2 * NO
    for c in range(2):
        block = green_ref[c]
        block_t = block.T
        for a in range(NEW):
            for k in range(times):
                at = ((a * times + k) * 2 + c) * NO
                g_out[at : at + NO, :] = block[a * NO : (a + 1) * NO, k * NO : (k + 1) * NO].astype(BF16)
                g_in[at : at + NO, :] = block_t[k * NO : (k + 1) * NO, a * NO : (a + 1) * NO].astype(BF16)

    rows = pairs * width

    def left(step, carry):
        lanes = pl.ds(pl.multiple_of(step * 2 * aux, 2 * aux), 2 * aux)
        res = mm(g_in[...], inner_ref[:, lanes])
        spread[pl.ds(2 * step, rows, stride=PITCH), :] = res[:, :aux]
        spread[pl.ds(2 * step + 1, rows, stride=PITCH), :] = res[:, aux:]
        return carry

    lax.fori_loop(0, NO // 2, left, 0)

    def right(step, carry):
        at = pl.ds(pl.multiple_of(step * aux, aux), aux)
        k_ref[at, :] = mm_nt(outer_ref[at, :], g_out[...]).astype(BF16)
        return carry

    lax.fori_loop(0, NO, right, 0)

    for n in range(pairs):

        def bubble(step, acc):
            lhs, rhs = [], []
            for d in range(2):
                m = 2 * step + d
                for c in range(2):
                    at = pl.multiple_of(((n * 2 + c) * NO + m) * PITCH, 8)
                    rhs.append(spread[pl.ds(at, NO), :].astype(BF16))
                m_ref[n * NO + m] = jnp.concatenate(rhs[-2:], axis=0)
                lhs.append(k_ref[pl.ds(pl.multiple_of(m * aux, aux), aux), n * width : (n + 1) * width])
            return acc + mm(jnp.concatenate(lhs, axis=1), jnp.concatenate(rhs, axis=0))

        acc = lax.fori_loop(0, NO // 2, bubble, jnp.zeros((aux, aux), F32), unroll=4)
        pi_ref[n * aux : (n + 1) * aux, :] = (acc.T * (1.0 / NO)).astype(BF16)

    def screen(step, carry):
        lanes = pl.ds(pl.multiple_of(step * 256, 256), 256)
        w_ref[:, lanes] = mm(pi_ref[...], fit_ref[:, lanes]).astype(BF16)
        return carry

    lax.fori_loop(0, NO * NO // 256, screen, 0)

    scale = (aux * NO) ** (-0.5)
    for a in range(NEW):
        outs = []
        for k in range(times):
            n = a * times + k

            def final(step, acc):
                at = n * NO + 4 * step
                even = jnp.concatenate([m_ref[at], m_ref[at + 2]], axis=1)
                odd = jnp.concatenate([m_ref[at + 1], m_ref[at + 3]], axis=1)
                w = [
                    w_ref[n * aux : (n + 1) * aux, pl.ds(pl.multiple_of((2 * step + d) * width, width), width)]
                    for d in range(2)
                ]
                return acc + mm(jnp.concatenate([even, odd], axis=0), jnp.concatenate(w, axis=0))

            acc = lax.fori_loop(0, NO // 4, final, jnp.zeros((2 * width, width), F32), unroll=2)
            outs.append((acc[:width, :NO] + acc[width:, NO:]) * scale)
        whole = jnp.concatenate(outs, axis=1).astype(BF16)
        for c in range(2):
            at = (c * NEW + a) * NO
            energy_ref[at : at + NO, :] = whole[c * NO : (c + 1) * NO]


def collide_kernel(rows_n, cols_n, energy_ref, start_ref, hist_ref, out_ref, seg, part, got, gs_sem, gr_sem, ss_sem, sr_sem):
    row, col = lax.axis_index("row"), lax.axis_index("col")
    span = energy_ref.shape[1]
    half = energy_ref.shape[0] // 2
    mine = row * cols_n + col
    source_col = mine // rows_n

    def owner(m):
        t = col * rows_n + m
        return t // cols_n, lax.rem(t, cols_n)

    barrier = pltpu.get_barrier_semaphore()
    for d in range(1, cols_n):
        pl.semaphore_signal(
            barrier, inc=1, device_id={"row": row, "col": lax.rem(col + d, cols_n)}, device_id_type=MESH
        )
    for r in range(rows_n):

        @pl.when(jnp.logical_or(row != r, col != source_col))
        def _():
            pl.semaphore_signal(barrier, inc=1, device_id={"row": r, "col": source_col}, device_id_type=MESH)

    keeps = jnp.where(source_col == col, 1, 0)
    pl.semaphore_wait(barrier, cols_n - 1 + rows_n - keeps)

    def gather(d):
        return pltpu.make_async_remote_copy(
            src_ref=energy_ref,
            dst_ref=seg.at[col],
            send_sem=gs_sem.at[d],
            recv_sem=gr_sem.at[d],
            device_id={"row": row, "col": lax.rem(col + d, cols_n)},
            device_id_type=MESH,
        )

    sends = [gather(d) for d in range(1, cols_n)]
    for copy in sends:
        copy.start()
    seg[col] = energy_ref[...]
    for copy in sends:
        copy.wait_recv()
    real = [seg[s, :half, :] for s in range(cols_n)]
    imag = [seg[s, half:, :] for s in range(cols_n)]
    lhs = jnp.concatenate(
        [jnp.concatenate(real + [-x for x in imag], axis=1), jnp.concatenate(imag + real, axis=1)], axis=0
    )

    def scatter(m):
        to_row, to_col = owner(m)
        return pltpu.make_async_remote_copy(
            src_ref=part.at[m],
            dst_ref=got.at[row],
            send_sem=ss_sem.at[m],
            recv_sem=sr_sem.at[row],
            device_id={"row": to_row, "col": to_col},
            device_id_type=MESH,
        )

    def away(m):
        to_row, to_col = owner(m)
        return jnp.logical_or(to_row != row, to_col != col)

    for m in range(rows_n):
        value = mm(lhs, hist_ref[:, m * span : (m + 1) * span]).astype(BF16)
        part[m] = value

        @pl.when(away(m))
        def _():
            scatter(m).start()

        @pl.when(jnp.logical_not(away(m)))
        def _():
            got[row] = value

    for r in range(rows_n):

        @pl.when(jnp.logical_or(row != r, col != source_col))
        def _():
            pltpu.make_async_remote_copy(
                src_ref=part.at[r],
                dst_ref=got.at[r],
                send_sem=ss_sem.at[r],
                recv_sem=sr_sem.at[r],
                device_id={"row": r, "col": source_col},
                device_id_type=MESH,
            ).wait_recv()

    total = got[0].astype(F32)
    for r in range(1, rows_n):
        total = total + got[r].astype(F32)
    out_ref[...] = start_ref[...] + total
    for copy in sends:
        copy.wait_send()
    for m in range(rows_n):

        @pl.when(away(m))
        def _():
            scatter(m).wait_send()


def local(green, fit, history):
    rows_n, cols_n = lax.axis_size("row"), lax.axis_size("col")
    aux = fit.shape[0]
    slice_rows, span = green.shape[1], green.shape[2]
    pairs = NEW * (span // NO)
    wide = pltpu.CompilerParams(vmem_limit_bytes=62 << 20)
    inner, outer = pl.pallas_call(
        prep_kernel,
        out_shape=(
            jax.ShapeDtypeStruct((NO, NO * aux), BF16),
            jax.ShapeDtypeStruct((NO * aux, NO), BF16),
        ),
        in_specs=[VMEM],
        out_specs=(VMEM, VMEM),
        scratch_shapes=[pltpu.VMEM((NO * PITCH, aux), F32)],
        name="prep",
    )(fit)
    energy = pl.pallas_call(
        energy_kernel,
        out_shape=jax.ShapeDtypeStruct((2 * slice_rows, span), BF16),
        in_specs=[VMEM] * 4,
        out_specs=VMEM,
        scratch_shapes=[
            pltpu.VMEM((pairs * 2 * NO, NO), BF16),
            pltpu.VMEM((pairs * 2 * NO, NO), BF16),
            pltpu.VMEM((pairs * 2 * NO * PITCH, aux), F32),
            pltpu.VMEM((pairs * NO, 2 * NO, aux), BF16),
            pltpu.VMEM((NO * aux, pairs * 2 * NO), BF16),
            pltpu.VMEM((pairs * aux, aux), BF16),
            pltpu.VMEM((pairs * aux, NO * NO), BF16),
        ],
        compiler_params=wide,
        name="energy",
    )
    collide = pl.pallas_call(
        functools.partial(collide_kernel, rows_n, cols_n),
        out_shape=jax.ShapeDtypeStruct((2 * slice_rows, span), F32),
        in_specs=[VMEM] * 3,
        out_specs=VMEM,
        scratch_shapes=[
            pltpu.VMEM((cols_n, 2 * slice_rows, span), BF16),
            pltpu.VMEM((rows_n, 2 * slice_rows, span), BF16),
            pltpu.VMEM((rows_n, 2 * slice_rows, span), BF16),
            pltpu.SemaphoreType.DMA((cols_n,)),
            pltpu.SemaphoreType.DMA((cols_n,)),
            pltpu.SemaphoreType.DMA((rows_n,)),
            pltpu.SemaphoreType.DMA((rows_n,)),
        ],
        compiler_params=pltpu.CompilerParams(
            collective_id=0, has_side_effects=True, vmem_limit_bytes=62 << 20
        ),
        name="collide",
    )
    start = green.reshape(2 * slice_rows, span)
    stacked = history.reshape(2 * history.shape[1], history.shape[2])
    current = start
    for _ in range(ITERS):
        sigma = energy(current.reshape(green.shape), fit, inner, outer)
        current = collide(sigma, start, stacked)
    return current.reshape(green.shape)


def solution(mesh):
    in_specs = (P("groups", None, ("row", "col")), P("groups", None), P("groups", "row", "col"))
    out_specs = P("groups", None, ("row", "col"))
    return jax.shard_map(local, mesh=mesh, in_specs=in_specs, out_specs=out_specs, check_vma=False)
```

```python
import functools

import jax
import jax.numpy as jnp
from jax import lax
from jax.experimental import pallas as pl
from jax.experimental.pallas import tpu as pltpu
from jax.sharding import PartitionSpec as P

NO = 64
NEW = 2
ITERS = 2
PITCH = NO + 8
UL, UR, UB, US, UF = 16, 4, 2, 16, 2
RB, BB, FB = 16, 32, 16
F32 = jnp.float32
BF16 = jnp.bfloat16
MESH = pl.DeviceIdType.MESH
VMEM = pl.BlockSpec(memory_space=pltpu.VMEM)


def mm(a, b):
    return jnp.dot(a, b, preferred_element_type=F32)


def mm_nt(a, b):
    return lax.dot_general(a, b, (((1,), (1,)), ((), ())), preferred_element_type=F32)


def prep_kernel(fit_ref, inner_ref, outer_ref, turned):
    aux = fit_ref.shape[0]
    for pair in range(NO // 2):
        block = fit_ref[:, pair * 2 * NO : (pair + 1) * 2 * NO].astype(F32).T
        for half in range(2):
            i = 2 * pair + half
            piece = block[half * NO : (half + 1) * NO]
            inner_ref[:, i * aux : (i + 1) * aux] = piece.astype(BF16)
            turned[i * PITCH : i * PITCH + NO, :] = piece
    for j in range(NO):
        piece = turned[pl.ds(j, NO, stride=PITCH), :]
        outer_ref[j * aux : (j + 1) * aux, :] = piece.T.astype(BF16)


def energy_kernel(green_ref, fit_ref, inner_ref, outer_ref, energy_ref, g_in, g_out, spread, m_ref, k_ref, pi_ref, w_ref):
    aux = fit_ref.shape[0]
    times = green_ref.shape[2] // NO
    pairs = NEW * times
    width = 2 * NO
    for c in range(2):
        block = green_ref[c]
        block_t = block.T
        for a in range(NEW):
            for k in range(times):
                at = ((a * times + k) * 2 + c) * NO
                g_out[at : at + NO, :] = block[a * NO : (a + 1) * NO, k * NO : (k + 1) * NO].astype(BF16)
                g_in[at : at + NO, :] = block_t[k * NO : (k + 1) * NO, a * NO : (a + 1) * NO].astype(BF16)

    rows = pairs * width

    def left(step, carry):
        lanes = pl.ds(pl.multiple_of(step * 2 * aux, 2 * aux), 2 * aux)
        res = mm(g_in[...], inner_ref[:, lanes])
        spread[pl.ds(2 * step, rows, stride=PITCH), :] = res[:, :aux]
        spread[pl.ds(2 * step + 1, rows, stride=PITCH), :] = res[:, aux:]
        return carry

    lax.fori_loop(0, NO // 2, left, 0, unroll=UL)

    def right(step, carry):
        at = pl.ds(pl.multiple_of(step * RB * aux, aux), RB * aux)
        k_ref[at, :] = mm_nt(outer_ref[at, :], g_out[...]).astype(BF16)
        return carry

    lax.fori_loop(0, NO // RB, right, 0, unroll=UR)

    for n in range(pairs):

        def bubble(step, acc):
            lhs, rhs = [], []
            for d in range(BB):
                m = BB * step + d
                for c in range(2):
                    at = pl.multiple_of(((n * 2 + c) * NO + m) * PITCH, 8)
                    rhs.append(spread[pl.ds(at, NO), :].astype(BF16))
                m_ref[n * NO + m] = jnp.concatenate(rhs[-2:], axis=0)
                lhs.append(k_ref[pl.ds(pl.multiple_of(m * aux, aux), aux), n * width : (n + 1) * width])
            return acc + mm(jnp.concatenate(lhs, axis=1), jnp.concatenate(rhs, axis=0))

        acc = lax.fori_loop(0, NO // BB, bubble, jnp.zeros((aux, aux), F32), unroll=UB)
        pi_ref[n * aux : (n + 1) * aux, :] = (acc.T * (1.0 / NO)).astype(BF16)

    def screen(step, carry):
        lanes = pl.ds(pl.multiple_of(step * 256, 256), 256)
        w_ref[:, lanes] = mm(pi_ref[...], fit_ref[:, lanes]).astype(BF16)
        return carry

    lax.fori_loop(0, NO * NO // 256, screen, 0, unroll=US)

    scale = (aux * NO) ** (-0.5)
    for a in range(NEW):
        outs = []
        for k in range(times):
            n = a * times + k

            def final(step, acc):
                at = n * NO + 2 * FB * step
                even = jnp.concatenate([m_ref[at + 2 * d] for d in range(FB)], axis=1)
                odd = jnp.concatenate([m_ref[at + 2 * d + 1] for d in range(FB)], axis=1)
                w = [
                    w_ref[n * aux : (n + 1) * aux, pl.ds(pl.multiple_of((FB * step + d) * width, width), width)]
                    for d in range(FB)
                ]
                return acc + mm(jnp.concatenate([even, odd], axis=0), jnp.concatenate(w, axis=0))

            acc = lax.fori_loop(0, NO // (2 * FB), final, jnp.zeros((2 * width, width), F32), unroll=UF)
            outs.append((acc[:width, :NO] + acc[width:, NO:]) * scale)
        whole = jnp.concatenate(outs, axis=1).astype(BF16)
        for c in range(2):
            at = (c * NEW + a) * NO
            energy_ref[at : at + NO, :] = whole[c * NO : (c + 1) * NO]


def collide_kernel(rows_n, cols_n, energy_ref, start_ref, hist_ref, out_ref, seg, part, got, gs_sem, gr_sem, ss_sem, sr_sem):
    row, col = lax.axis_index("row"), lax.axis_index("col")
    span = energy_ref.shape[1]
    half = energy_ref.shape[0] // 2
    mine = row * cols_n + col
    source_col = mine // rows_n

    def owner(m):
        t = col * rows_n + m
        return t // cols_n, lax.rem(t, cols_n)

    barrier = pltpu.get_barrier_semaphore()
    for d in range(1, cols_n):
        pl.semaphore_signal(
            barrier, inc=1, device_id={"row": row, "col": lax.rem(col + d, cols_n)}, device_id_type=MESH
        )
    for r in range(rows_n):

        @pl.when(jnp.logical_or(row != r, col != source_col))
        def _():
            pl.semaphore_signal(barrier, inc=1, device_id={"row": r, "col": source_col}, device_id_type=MESH)

    keeps = jnp.where(source_col == col, 1, 0)
    pl.semaphore_wait(barrier, cols_n - 1 + rows_n - keeps)

    def gather(d):
        return pltpu.make_async_remote_copy(
            src_ref=energy_ref,
            dst_ref=seg.at[col],
            send_sem=gs_sem.at[d],
            recv_sem=gr_sem.at[d],
            device_id={"row": row, "col": lax.rem(col + d, cols_n)},
            device_id_type=MESH,
        )

    sends = [gather(d) for d in range(1, cols_n)]
    for copy in sends:
        copy.start()
    seg[col] = energy_ref[...]
    for copy in sends:
        copy.wait_recv()
    real = [seg[s, :half, :] for s in range(cols_n)]
    imag = [seg[s, half:, :] for s in range(cols_n)]
    lhs = jnp.concatenate(
        [jnp.concatenate(real + [-x for x in imag], axis=1), jnp.concatenate(imag + real, axis=1)], axis=0
    )

    def scatter(m):
        to_row, to_col = owner(m)
        return pltpu.make_async_remote_copy(
            src_ref=part.at[m],
            dst_ref=got.at[row],
            send_sem=ss_sem.at[m],
            recv_sem=sr_sem.at[row],
            device_id={"row": to_row, "col": to_col},
            device_id_type=MESH,
        )

    def away(m):
        to_row, to_col = owner(m)
        return jnp.logical_or(to_row != row, to_col != col)

    for m in range(rows_n):
        value = mm(lhs, hist_ref[:, m * span : (m + 1) * span]).astype(BF16)
        part[m] = value

        @pl.when(away(m))
        def _():
            scatter(m).start()

        @pl.when(jnp.logical_not(away(m)))
        def _():
            got[row] = value

    for r in range(rows_n):

        @pl.when(jnp.logical_or(row != r, col != source_col))
        def _():
            pltpu.make_async_remote_copy(
                src_ref=part.at[r],
                dst_ref=got.at[r],
                send_sem=ss_sem.at[r],
                recv_sem=sr_sem.at[r],
                device_id={"row": r, "col": source_col},
                device_id_type=MESH,
            ).wait_recv()

    total = got[0].astype(F32)
    for r in range(1, rows_n):
        total = total + got[r].astype(F32)
    out_ref[...] = start_ref[...] + total
    for copy in sends:
        copy.wait_send()
    for m in range(rows_n):

        @pl.when(away(m))
        def _():
            scatter(m).wait_send()


def local(green, fit, history):
    rows_n, cols_n = lax.axis_size("row"), lax.axis_size("col")
    aux = fit.shape[0]
    slice_rows, span = green.shape[1], green.shape[2]
    pairs = NEW * (span // NO)
    wide = pltpu.CompilerParams(vmem_limit_bytes=62 << 20)
    inner, outer = pl.pallas_call(
        prep_kernel,
        out_shape=(
            jax.ShapeDtypeStruct((NO, NO * aux), BF16),
            jax.ShapeDtypeStruct((NO * aux, NO), BF16),
        ),
        in_specs=[VMEM],
        out_specs=(VMEM, VMEM),
        scratch_shapes=[pltpu.VMEM((NO * PITCH, aux), F32)],
        name="prep",
    )(fit)
    energy = pl.pallas_call(
        energy_kernel,
        out_shape=jax.ShapeDtypeStruct((2 * slice_rows, span), BF16),
        in_specs=[VMEM] * 4,
        out_specs=VMEM,
        scratch_shapes=[
            pltpu.VMEM((pairs * 2 * NO, NO), BF16),
            pltpu.VMEM((pairs * 2 * NO, NO), BF16),
            pltpu.VMEM((pairs * 2 * NO * PITCH, aux), F32),
            pltpu.VMEM((pairs * NO, 2 * NO, aux), BF16),
            pltpu.VMEM((NO * aux, pairs * 2 * NO), BF16),
            pltpu.VMEM((pairs * aux, aux), BF16),
            pltpu.VMEM((pairs * aux, NO * NO), BF16),
        ],
        compiler_params=wide,
        name="energy",
    )
    collide = pl.pallas_call(
        functools.partial(collide_kernel, rows_n, cols_n),
        out_shape=jax.ShapeDtypeStruct((2 * slice_rows, span), F32),
        in_specs=[VMEM] * 3,
        out_specs=VMEM,
        scratch_shapes=[
            pltpu.VMEM((cols_n, 2 * slice_rows, span), BF16),
            pltpu.VMEM((rows_n, 2 * slice_rows, span), BF16),
            pltpu.VMEM((rows_n, 2 * slice_rows, span), BF16),
            pltpu.SemaphoreType.DMA((cols_n,)),
            pltpu.SemaphoreType.DMA((cols_n,)),
            pltpu.SemaphoreType.DMA((rows_n,)),
            pltpu.SemaphoreType.DMA((rows_n,)),
        ],
        compiler_params=pltpu.CompilerParams(
            collective_id=0, has_side_effects=True, vmem_limit_bytes=62 << 20
        ),
        name="collide",
    )
    start = green.reshape(2 * slice_rows, span)
    stacked = history.reshape(2 * history.shape[1], history.shape[2])
    current = start
    for _ in range(ITERS):
        sigma = energy(current.reshape(green.shape), fit, inner, outer)
        current = collide(sigma, start, stacked)
    return current.reshape(green.shape)


def solution(mesh):
    in_specs = (P("groups", None, ("row", "col")), P("groups", None), P("groups", "row", "col"))
    out_specs = P("groups", None, ("row", "col"))
    return jax.shard_map(local, mesh=mesh, in_specs=in_specs, out_specs=out_specs, check_vma=False)
```

```python
import functools

import jax
import jax.numpy as jnp
from jax import lax
from jax.experimental import pallas as pl
from jax.experimental.pallas import tpu as pltpu
from jax.sharding import PartitionSpec as P

NO = 64
NEW = 2
ITERS = 2
PITCH = NO + 8
UL, UR, UB, US, UF = 16, 4, 2, 16, 2
RB, BB, FB = 16, 32, 16
F32 = jnp.float32
BF16 = jnp.bfloat16
MESH = pl.DeviceIdType.MESH
VMEM = pl.BlockSpec(memory_space=pltpu.VMEM)


def mm(a, b):
    return jnp.dot(a, b, preferred_element_type=F32)


def mm_nt(a, b):
    return lax.dot_general(a, b, (((1,), (1,)), ((), ())), preferred_element_type=F32)


def prepare(fit_ref, inner_ref, outer_ref, turned):
    aux = fit_ref.shape[0]
    for pair in range(NO // 2):
        block = fit_ref[:, pair * 2 * NO : (pair + 1) * 2 * NO].astype(F32).T
        for half in range(2):
            i = 2 * pair + half
            piece = block[half * NO : (half + 1) * NO]
            inner_ref[:, i * aux : (i + 1) * aux] = piece.astype(BF16)
            turned[i * PITCH : i * PITCH + NO, :] = piece
    for j in range(NO):
        piece = turned[pl.ds(j, NO, stride=PITCH), :]
        outer_ref[j * aux : (j + 1) * aux, :] = piece.T.astype(BF16)


def products(a, now_ref, inner_ref, outer_ref, g_in, g_out, spread, k_ref):
    aux = inner_ref.shape[1] // NO
    times = now_ref.shape[2] // NO
    rows = times * 2 * NO
    for c in range(2):
        block = now_ref[c, a * NO : (a + 1) * NO, :]
        block_t = block.T
        for n in range(times):
            at = (n * 2 + c) * NO
            g_out[at : at + NO, :] = block[:, n * NO : (n + 1) * NO].astype(BF16)
            g_in[at : at + NO, :] = block_t[n * NO : (n + 1) * NO, :].astype(BF16)

    def left(step, carry):
        lanes = pl.ds(pl.multiple_of(step * 2 * aux, 2 * aux), 2 * aux)
        res = mm(g_in[...], inner_ref[:, lanes])
        spread[pl.ds(2 * step, rows, stride=PITCH), :] = res[:, :aux]
        spread[pl.ds(2 * step + 1, rows, stride=PITCH), :] = res[:, aux:]
        return carry

    lax.fori_loop(0, NO // 2, left, 0, unroll=UL)

    def right(step, carry):
        at = pl.ds(pl.multiple_of(step * RB * aux, aux), RB * aux)
        k_ref[at, :] = mm_nt(outer_ref[at, :], g_out[...]).astype(BF16)
        return carry

    lax.fori_loop(0, NO // RB, right, 0, unroll=UR)


def contract(times, fit_ref, spread, m_ref, k_ref, pi_ref, w_ref):
    aux = fit_ref.shape[0]
    width = 2 * NO
    for n in range(times):

        def bubble(step, acc):
            lhs, rhs = [], []
            for d in range(BB):
                m = BB * step + d
                for c in range(2):
                    at = pl.multiple_of(((n * 2 + c) * NO + m) * PITCH, 8)
                    rhs.append(spread[pl.ds(at, NO), :].astype(BF16))
                m_ref[n * NO + m] = jnp.concatenate(rhs[-2:], axis=0)
                lhs.append(k_ref[pl.ds(pl.multiple_of(m * aux, aux), aux), n * width : (n + 1) * width])
            return acc + mm(jnp.concatenate(lhs, axis=1), jnp.concatenate(rhs, axis=0))

        acc = lax.fori_loop(0, NO // BB, bubble, jnp.zeros((aux, aux), F32), unroll=UB)
        pi_ref[n * aux : (n + 1) * aux, :] = (acc.T * (1.0 / NO)).astype(BF16)

    def screen(step, carry):
        lanes = pl.ds(pl.multiple_of(step * 256, 256), 256)
        w_ref[:, lanes] = mm(pi_ref[...], fit_ref[:, lanes]).astype(BF16)
        return carry

    lax.fori_loop(0, NO * NO // 256, screen, 0, unroll=US)

    scale = (aux * NO) ** (-0.5)
    outs = []
    for n in range(times):

        def final(step, acc):
            at = n * NO + 2 * FB * step
            even = jnp.concatenate([m_ref[at + 2 * d] for d in range(FB)], axis=1)
            odd = jnp.concatenate([m_ref[at + 2 * d + 1] for d in range(FB)], axis=1)
            w = [
                w_ref[n * aux : (n + 1) * aux, pl.ds(pl.multiple_of((FB * step + d) * width, width), width)]
                for d in range(FB)
            ]
            return acc + mm(jnp.concatenate([even, odd], axis=0), jnp.concatenate(w, axis=0))

        acc = lax.fori_loop(0, NO // (2 * FB), final, jnp.zeros((2 * width, width), F32), unroll=UF)
        outs.append((acc[:width, :NO] + acc[width:, NO:]) * scale)
    return jnp.concatenate(outs, axis=1).astype(BF16)


def whole_kernel(
    rows_n, cols_n, green_ref, fit_ref, hist_ref, out_ref,
    inner, outer, turned, g_in, g_out, spread, m_ref, k_ref, pi_ref, w_ref,
    now, energy, seg, part, got, gs_sem, gr_sem, ss_sem, sr_sem,
):
    row, col = lax.axis_index("row"), lax.axis_index("col")
    span = green_ref.shape[2]
    times = span // NO
    source_col = (row * cols_n + col) // rows_n

    def owner(m):
        t = col * rows_n + m
        return t // cols_n, lax.rem(t, cols_n)

    def away(m):
        to_row, to_col = owner(m)
        return jnp.logical_or(to_row != row, to_col != col)

    def foreign(r):
        return jnp.logical_or(row != r, col != source_col)

    def place(r, c):
        return {"row": r, "col": c}

    barrier = pltpu.get_barrier_semaphore()
    for d in range(1, cols_n):
        pl.semaphore_signal(barrier, inc=1, device_id=place(row, lax.rem(col + d, cols_n)), device_id_type=MESH)
    for r in range(rows_n):

        @pl.when(foreign(r))
        def _():
            pl.semaphore_signal(barrier, inc=1, device_id=place(r, source_col), device_id_type=MESH)

    prepare(fit_ref, inner, outer, turned)

    keeps = jnp.where(source_col == col, 1, 0)
    pl.semaphore_wait(barrier, cols_n - 1 + rows_n - keeps)

    def gather(s, d):
        return pltpu.make_async_remote_copy(
            src_ref=energy.at[s],
            dst_ref=seg.at[s, col],
            send_sem=gs_sem.at[s, d],
            recv_sem=gr_sem.at[s, d],
            device_id=place(row, lax.rem(col + d, cols_n)),
            device_id_type=MESH,
        )

    def scatter(s, m):
        return pltpu.make_async_remote_copy(
            src_ref=part.at[s, m],
            dst_ref=got.at[s, row],
            send_sem=ss_sem.at[s, m],
            recv_sem=sr_sem.at[s, row],
            device_id=place(*owner(m)),
            device_id_type=MESH,
        )

    def arriving(s, r):
        return pltpu.make_async_remote_copy(
            src_ref=part.at[s, r],
            dst_ref=got.at[s, r],
            send_sem=ss_sem.at[s, r],
            recv_sem=sr_sem.at[s, r],
            device_id=place(r, source_col),
            device_id_type=MESH,
        )

    def multiply(s):
        for d in range(1, cols_n):
            gather(s, d).wait_recv()
        real = [seg[s, q, :NO, :] for q in range(cols_n)]
        imag = [seg[s, q, NO:, :] for q in range(cols_n)]
        lhs = jnp.concatenate(
            [jnp.concatenate(real + [-x for x in imag], axis=1), jnp.concatenate(imag + real, axis=1)], axis=0
        )
        for m in range(rows_n):
            value = mm(lhs, hist_ref[:, m * span : (m + 1) * span]).astype(BF16)
            part[s, m] = value

            @pl.when(away(m))
            def _():
                scatter(s, m).start()

            @pl.when(jnp.logical_not(away(m)))
            def _():
                got[s, row] = value

    def collect(s, target):
        a = s % NEW
        for r in range(rows_n):

            @pl.when(foreign(r))
            def _():
                arriving(s, r).wait_recv()

        total = got[s, 0].astype(F32)
        for r in range(1, rows_n):
            total = total + got[s, r].astype(F32)
        for c in range(2):
            at = slice(a * NO, (a + 1) * NO)
            target[c, at, :] = green_ref[c, at, :] + total[c * NO : (c + 1) * NO]

    steps = ITERS * NEW
    for s in range(steps):
        a = s % NEW
        if s >= NEW:
            collect(s - NEW, now)
        products(a, green_ref if s < NEW else now, inner, outer, g_in, g_out, spread, k_ref)
        if s >= 1:
            multiply(s - 1)
        value = contract(times, fit_ref, spread, m_ref, k_ref, pi_ref, w_ref)
        energy[s] = value
        for d in range(1, cols_n):
            gather(s, d).start()
        seg[s, col] = value
    multiply(steps - 1)
    for s in range(steps - NEW, steps):
        collect(s, out_ref)
    for s in range(steps):
        for d in range(1, cols_n):
            gather(s, d).wait_send()
        for m in range(rows_n):

            @pl.when(away(m))
            def _():
                scatter(s, m).wait_send()


def local(green, fit, history):
    rows_n, cols_n = lax.axis_size("row"), lax.axis_size("col")
    aux = fit.shape[0]
    span = green.shape[2]
    times = span // NO
    steps = ITERS * NEW
    stacked = history.reshape(2 * history.shape[1], history.shape[2])
    block = (2 * NO, span)
    return pl.pallas_call(
        functools.partial(whole_kernel, rows_n, cols_n),
        out_shape=jax.ShapeDtypeStruct(green.shape, F32),
        in_specs=[VMEM] * 3,
        out_specs=VMEM,
        scratch_shapes=[
            pltpu.VMEM((NO, NO * aux), BF16),
            pltpu.VMEM((NO * aux, NO), BF16),
            pltpu.VMEM((NO * PITCH, aux), F32),
            pltpu.VMEM((times * 2 * NO, NO), BF16),
            pltpu.VMEM((times * 2 * NO, NO), BF16),
            pltpu.VMEM((times * 2 * NO * PITCH, aux), F32),
            pltpu.VMEM((times * NO, 2 * NO, aux), BF16),
            pltpu.VMEM((NO * aux, times * 2 * NO), BF16),
            pltpu.VMEM((times * aux, aux), BF16),
            pltpu.VMEM((times * aux, NO * NO), BF16),
            pltpu.VMEM(green.shape, F32),
            pltpu.VMEM((steps, *block), BF16),
            pltpu.VMEM((steps, cols_n, *block), BF16),
            pltpu.VMEM((steps, rows_n, *block), BF16),
            pltpu.VMEM((steps, rows_n, *block), BF16),
            pltpu.SemaphoreType.DMA((steps, cols_n)),
            pltpu.SemaphoreType.DMA((steps, cols_n)),
            pltpu.SemaphoreType.DMA((steps, rows_n)),
            pltpu.SemaphoreType.DMA((steps, rows_n)),
        ],
        compiler_params=pltpu.CompilerParams(
            collective_id=0, has_side_effects=True, vmem_limit_bytes=62 << 20
        ),
        name="whole",
    )(green, fit, stacked)


def solution(mesh):
    in_specs = (P("groups", None, ("row", "col")), P("groups", None), P("groups", "row", "col"))
    out_specs = P("groups", None, ("row", "col"))
    return jax.shard_map(local, mesh=mesh, in_specs=in_specs, out_specs=out_specs, check_vma=False)
```
